512 devices in a mesh: group: 16 (over y, x), member: 32 (over z, core).
Axes of the slice: x: 4, y: 4, z: 16, core: 2. Of those that a mesh axis runs over, the one named last changes fastest.
Arguments:
- amplitudes: bfloat16 [8192, 128, 128], P(('group', 'member')), may hold values from -6 to 6
- integrals: bfloat16 [4096, 128, 128], P(('group', 'member')), may hold values from -0.02734375 to 0.02734375
- tasks: int32 [196608, 3], P(('group', 'member')), may hold values from 0 to 63, as said below
- requests: int32 [8192, 4], P(('group', 'member')), may hold values from 0 to 7
- counts: int32 [512], P(('group', 'member')), may hold values from 1 to 384, as said below
Outputs:
- residual: float32 [512, 128, 128], P(('group', 'member'))
The draws below stay inside these ranges and needn't reach their ends.
Inputs may be any that keep to these rules, and one draw needn't show every extreme that they name: `tasks`: column 0 is below 16, column 1 below 64, column 2 below 32; slots beyond a device's count hold valid entries too. `counts`: some device has 384 live tasks in every draw.
All inputs are finite; a program needn't handle non-finite values.
Results may differ from the reference program's by a relative error of at most 0.0003.
Values may be sent and summed in bfloat16 or wider, within the bound.
No kernel may reach another device: no remote copies, remote signals or barrier semaphores. Data moves between devices by JAX's collectives and lax.ppermute only.
A program may use at most 64 MiB of HBM per device.

```python
import jax
import jax.numpy as jnp
from jax import lax

TILE = 128
AMP_DEV = 16
V_DEV = 8
FETCH_CAP = 4
TASK_CAP = 384
FETCH_SLOTS = 64
RES_GROUP = 32
AMPS = 8192
VTILES = 4096
TASKS = 196608
REQ_ROWS = 8192
RTILES = 512
N_GROUP = 16
N_MEMBER = 32
DEVICES = 512


def draw_tasks(key, part):
    first = jax.random.randint(jax.random.fold_in(key, 11), (TASKS,), 0, AMP_DEV)
    second = jax.random.randint(jax.random.fold_in(key, 12), (TASKS,), 0, FETCH_SLOTS)
    third = jax.random.randint(jax.random.fold_in(key, 13), (TASKS,), 0, RES_GROUP)
    return jnp.stack([first, second, third], axis=1).astype(jnp.int32)


def draw_counts(key, part):
    shifts = jax.random.randint(jax.random.fold_in(key, 21), (DEVICES,), 0, 4)
    base = jnp.right_shift(jnp.full((DEVICES,), TASK_CAP, jnp.int32), shifts.astype(jnp.int32))
    jitter = jax.random.randint(jax.random.fold_in(key, 22), (DEVICES,), 0, base // 2 + 1)
    values = base - jitter
    chosen = jax.random.randint(jax.random.fold_in(key, 23), (), 0, DEVICES)
    values = jnp.where(jnp.arange(DEVICES) == chosen, TASK_CAP, values)
    return values.astype(jnp.int32)


def plant(entries, rng, low, high):
    longest = entries.shape.index(max(entries.shape))
    spots = []
    for shift in (0, 1):
        where = [jax.random.randint(jax.random.fold_in(rng, axis), (), 0, length) for axis, length in enumerate(entries.shape)]
        where[longest] = (where[longest] + shift) % entries.shape[longest]
        spots.append(tuple(where))
    return entries.at[spots[0]].set(low).at[spots[1]].set(high)


def block_scale(key, shape, pieces, smallest, largest):
    loudness = 1.0
    for axis_at, shards_of in pieces:
        steps = jax.random.uniform(jax.random.fold_in(jax.random.fold_in(key, 6), axis_at), (shards_of,), jnp.float32, smallest / len(pieces), largest / len(pieces))
        loudness = loudness * jnp.repeat(jnp.exp(steps), shape[axis_at] // shards_of).reshape((-1,) + (1,) * (len(shape) - 1 - axis_at))
    return loudness


def noise(key, dims, scale, most, pieces=(), kind=jnp.bfloat16):
    values = scale * jax.random.normal(key, dims, jnp.float32)
    if pieces:
        values = values * block_scale(key, dims, pieces, -0.22, 0.18)
    return jnp.clip(values, -most, most).astype(kind)


def setup_inputs(seed: int = 0) -> dict:
    keys = jax.random.split(jax.random.key(seed), 6)
    return {
        "amplitudes": noise(keys[0], (AMPS, TILE, TILE), 1.0, 6.0, ((0, 512),)),
        "integrals": noise(keys[1], (VTILES, TILE, TILE), (TILE * TASK_CAP) ** -0.5, 0.02734375, ((0, 512),)),
        "tasks": draw_tasks(jax.random.fold_in(keys[5], 71), 0),
        "requests": plant(jax.random.randint(keys[3], (REQ_ROWS, FETCH_CAP), 0, V_DEV), jax.random.fold_in(keys[3], 1), 0, V_DEV - 1).astype(jnp.int32),
        "counts": draw_counts(jax.random.fold_in(keys[5], 71), 0),
    }


def reference(amplitudes, integrals, tasks, requests, counts):
    tile = amplitudes.shape[1]

    def device(d, result):
        d = jnp.asarray(d).astype(jnp.int32)
        group_index = d // N_MEMBER
        member_index = d % N_MEMBER
        amps = lax.dynamic_slice_in_dim(amplitudes, d * AMP_DEV, AMP_DEV, 0)
        wanted = lax.dynamic_slice_in_dim(requests, d * N_GROUP, N_GROUP, 0)
        column = jnp.arange(N_GROUP, dtype=jnp.int32)[:, None] * N_MEMBER + member_index
        index = ((column * V_DEV + wanted).reshape(-1)).astype(jnp.int32)
        fetched = integrals[index]
        own = lax.dynamic_slice_in_dim(tasks, d * TASK_CAP, TASK_CAP, 0)
        count = counts[d]

        def block(k, total):
            start = (jnp.asarray(k) * 16).astype(jnp.int32)
            rows = lax.dynamic_slice_in_dim(own, start, 16, 0)
            valid = (start + jnp.arange(16, dtype=jnp.int32)) < count
            left = amps[rows[:, 0]].astype(jnp.float32)
            right = fetched[rows[:, 1]].astype(jnp.float32)
            product = jnp.einsum("kij,kjl->kil", left, right)
            product = jnp.where(valid[:, None, None], product, jnp.zeros_like(product))
            target = (group_index * RES_GROUP + rows[:, 2]).astype(jnp.int32)
            return total.at[target].add(product)

        return lax.fori_loop(0, (count + 15) // 16, block, result)

    start_total = jnp.zeros((RTILES, tile, tile), jnp.float32)
    return lax.fori_loop(0, DEVICES, device, start_total)
```

```python
import functools

import jax
import jax.numpy as jnp
from jax import lax
from jax.experimental import pallas as pl
from jax.experimental.pallas import tpu as pltpu
from jax.sharding import Mesh
from jax.sharding import PartitionSpec as P

GROUP_MEMBER = ("group", "z", "core")
PAIR = 2
UNROLL = 8
SLOTS = 512
TOP = 32760.0
STEPS = 128.0


def task_tables(tasks, counts, core, tiles):
    a, s, r = tasks.T
    half = tiles // 2
    k = jnp.arange(tasks.shape[0], dtype=jnp.int32)
    valid = k < counts[0]
    q = jnp.where(valid, ((r & 1) ^ core ^ 1) * half + (r >> 1), tiles)
    code = a + s * 32
    rank = jnp.sum(((q[:, None] == q[None, :]) & (k[None, :] < k[:, None])).astype(jnp.int32), 1)
    b = jnp.arange(tiles, dtype=jnp.int32)
    hot = q[:, None] == b[None, :]
    groups = (jnp.sum(hot.astype(jnp.int32), 0) + PAIR - 1) // PAIR
    ends = jnp.sum(jnp.where(b[:, None] <= b[None, :], groups[:, None], 0), 0)
    first = jnp.sum(jnp.where(hot, (ends - groups)[None, :], 0), 1)
    place = jnp.where(valid, first * PAIR + rank, -1)
    p = jnp.arange(SLOTS, dtype=jnp.int32)
    table = 16 + jnp.sum(jnp.where(place[:, None] == p[None, :], code[:, None] - 16, 0), 0)
    j = jnp.arange(SLOTS // PAIR, dtype=jnp.int32)
    target = jnp.sum((ends[:, None] <= j[None, :]).astype(jnp.int32), 0)
    bounds = jnp.stack([jnp.zeros_like(ends[0]), ends[half - 1], ends[tiles - 1]])
    return table, target, bounds


def contract_kernel(which, half, table, target, bounds, amps, fetched, out, acc):
    low, high = bounds[which], bounds[which + 1]
    acc[...] = jnp.zeros_like(acc)

    def step(i, carry):
        products = []
        for u in range(UNROLL):
            j = low + i * UNROLL + u
            codes = [table[j * PAIR + n] for n in range(PAIR)]
            left = jnp.concatenate([amps[c & 31] for c in codes], axis=1)
            right = jnp.concatenate([fetched[c >> 5] for c in codes], axis=0)
            products.append(jnp.dot(left, right, preferred_element_type=jnp.float32))
        for u in range(UNROLL):
            j = low + i * UNROLL + u
            tile = jnp.where(j < high, target[j] - which * half, half)
            acc[tile] += products[u]
        return carry

    lax.fori_loop(0, (high - low + UNROLL - 1) // UNROLL, step, 0)
    out[...] = acc[:half]


def contract(which, tables, amps, fetched, half):
    size = amps.shape[1]
    full = lambda n: pl.BlockSpec((n, size, size), lambda i, *_: (0, 0, 0))
    return pl.pallas_call(
        functools.partial(contract_kernel, which, half),
        grid_spec=pltpu.PrefetchScalarGridSpec(
            num_scalar_prefetch=3,
            grid=(1,),
            in_specs=[full(amps.shape[0]), full(fetched.shape[0])],
            out_specs=full(half),
            scratch_shapes=[pltpu.VMEM((half + 1, size, size), jnp.float32)],
        ),
        out_shape=jax.ShapeDtypeStruct((half, size, size), jnp.float32),
        compiler_params=pltpu.CompilerParams(vmem_limit_bytes=40 << 20),
        cost_estimate=pl.CostEstimate(
            flops=1 << 32, bytes_accessed=4 << 20, transcendentals=0
        ),
        name="contract_%d" % which,
    )(*tables, amps, fetched)


def encode_kernel(own, other, out):
    size = own.shape[1]
    for i in range(own.shape[0]):
        v = own[i] + other[i]
        top = jnp.max(jnp.abs(v), axis=0, keepdims=True)
        scale = jnp.ceil(jnp.log2(jnp.maximum(top, 1e-32)) * STEPS + 0.01)
        codes = v * (jnp.exp2(scale * (-1.0 / STEPS)) * TOP)
        out[i, :size] = jnp.floor(codes + 0.5).astype(jnp.int32).astype(jnp.int16)
        row = jnp.broadcast_to(scale, (out.shape[1] - size, size))
        out[i, size:] = row.astype(jnp.int32).astype(jnp.int16)


def encode(own, other, block=4):
    tiles, size, _ = own.shape
    spec = lambda rows: pl.BlockSpec((block, rows, size), lambda i: (i, 0, 0))
    return pl.pallas_call(
        encode_kernel,
        grid=(tiles // block,),
        in_specs=[spec(size), spec(size)],
        out_specs=spec(size + 16),
        out_shape=jax.ShapeDtypeStruct((tiles, size + 16, size), jnp.int16),
        cost_estimate=pl.CostEstimate(flops=1 << 20, bytes_accessed=3 << 20, transcendentals=0),
        name="encode",
    )(own, other)


def decode_kernel(pieces, out):
    size = out.shape[1]
    total = jnp.zeros((size, size), jnp.float32)
    for i in range(pieces.shape[0]):
        scale = pieces[i, size:].astype(jnp.int32).astype(jnp.float32)[:1]
        codes = pieces[i, :size].astype(jnp.int32).astype(jnp.float32)
        total += codes * (jnp.exp2(scale * (1.0 / STEPS)) * (1.0 / TOP))
    out[0] = total


def decode(pieces):
    size = pieces.shape[2]
    return pl.pallas_call(
        decode_kernel,
        out_shape=jax.ShapeDtypeStruct((1, size, size), jnp.float32),
        cost_estimate=pl.CostEstimate(flops=1 << 20, bytes_accessed=1 << 20, transcendentals=0),
        name="decode",
    )(pieces)


def per_device(amplitudes, integrals, tasks, requests, counts):
    tile = amplitudes.shape[1]
    half = lax.axis_size("z")
    wanted = lax.all_to_all(requests, "group", split_axis=0, concat_axis=0, tiled=True)
    fetched = lax.all_to_all(
        integrals[wanted], "group", split_axis=0, concat_axis=0, tiled=True
    ).reshape(-1, tile, tile)
    tables = task_tables(tasks, counts, lax.axis_index("core"), 2 * half)
    amps = jnp.concatenate([amplitudes, jnp.zeros((1, tile, tile), amplitudes.dtype)])
    other = contract(0, tables, amps, fetched, half)
    other = lax.ppermute(other, "core", [(0, 1), (1, 0)])
    own = contract(1, tables, amps, fetched, half)
    pieces = lax.all_to_all(encode(own, other), "z", split_axis=0, concat_axis=0, tiled=True)
    return decode(pieces)


def solution(mesh):
    finer = Mesh(mesh.devices.reshape(mesh.shape["group"], 16, 2), GROUP_MEMBER)
    placed = (
        P(GROUP_MEMBER, None, None),
        P(GROUP_MEMBER, None, None),
        P(GROUP_MEMBER, None),
        P(GROUP_MEMBER, None),
        P(GROUP_MEMBER),
    )
    return jax.shard_map(
        per_device,
        mesh=finer,
        in_specs=placed,
        out_specs=P(GROUP_MEMBER, None, None),
        check_vma=False,
    )
```

```python
import functools

import jax
import jax.numpy as jnp
from jax import lax
from jax.experimental import pallas as pl
from jax.experimental.pallas import tpu as pltpu
from jax.sharding import Mesh
from jax.sharding import PartitionSpec as P

GROUP_MEMBER = ("group", "z", "core")
PAIR = 2
UNROLL = 8
SLOTS = 512
TOP = 32760.0
STEPS = 128.0


def select_kernel(wanted, tiles, out):
    for i in range(out.shape[0]):
        out[i] = tiles[wanted[i]]


def select(wanted, tiles):
    size = tiles.shape[1]
    full = lambda n: pl.BlockSpec((n, size, size), lambda i, *_: (0, 0, 0))
    return pl.pallas_call(
        select_kernel,
        grid_spec=pltpu.PrefetchScalarGridSpec(
            num_scalar_prefetch=1,
            grid=(1,),
            in_specs=[full(tiles.shape[0])],
            out_specs=full(wanted.shape[0]),
        ),
        out_shape=jax.ShapeDtypeStruct((wanted.shape[0], size, size), tiles.dtype),
        compiler_params=pltpu.CompilerParams(vmem_limit_bytes=16 << 20),
        cost_estimate=pl.CostEstimate(flops=0, bytes_accessed=2 << 20, transcendentals=0),
        name="select",
    )(wanted, tiles)


def task_tables(tasks, counts, core, tiles):
    a, s, r = tasks.T
    half = tiles // 2
    k = jnp.arange(tasks.shape[0], dtype=jnp.int32)
    valid = k < counts[0]
    q = jnp.where(valid, ((r & 1) ^ core ^ 1) * half + (r >> 1), tiles)
    code = a + s * 32
    rank = jnp.sum(((q[:, None] == q[None, :]) & (k[None, :] < k[:, None])).astype(jnp.int32), 1)
    b = jnp.arange(tiles, dtype=jnp.int32)
    hot = q[:, None] == b[None, :]
    groups = (jnp.sum(hot.astype(jnp.int32), 0) + PAIR - 1) // PAIR
    ends = jnp.sum(jnp.where(b[:, None] <= b[None, :], groups[:, None], 0), 0)
    first = jnp.sum(jnp.where(hot, (ends - groups)[None, :], 0), 1)
    place = jnp.where(valid, first * PAIR + rank, -1)
    p = jnp.arange(SLOTS, dtype=jnp.int32)
    table = 16 + jnp.sum(jnp.where(place[:, None] == p[None, :], code[:, None] - 16, 0), 0)
    j = jnp.arange(SLOTS // PAIR, dtype=jnp.int32)
    target = jnp.sum((ends[:, None] <= j[None, :]).astype(jnp.int32), 0)
    bounds = jnp.stack([jnp.zeros_like(ends[0]), ends[half - 1], ends[tiles - 1]])
    return table, target, bounds


def contract_kernel(which, half, table, target, bounds, amps, fetched, out, acc):
    low, high = bounds[which], bounds[which + 1]
    acc[...] = jnp.zeros_like(acc)

    def step(i, carry):
        products = []
        for u in range(UNROLL):
            j = low + i * UNROLL + u
            codes = [table[j * PAIR + n] for n in range(PAIR)]
            left = jnp.concatenate([amps[c & 31] for c in codes], axis=1)
            right = jnp.concatenate([fetched[c >> 5] for c in codes], axis=0)
            products.append(jnp.dot(left, right, preferred_element_type=jnp.float32))
        for u in range(UNROLL):
            j = low + i * UNROLL + u
            tile = jnp.where(j < high, target[j] - which * half, half)
            acc[tile] += products[u]
        return carry

    lax.fori_loop(0, (high - low + UNROLL - 1) // UNROLL, step, 0)
    out[...] = acc[:half]


def contract(which, tables, amps, fetched, half):
    size = amps.shape[1]
    full = lambda n: pl.BlockSpec((n, size, size), lambda i, *_: (0, 0, 0))
    return pl.pallas_call(
        functools.partial(contract_kernel, which, half),
        grid_spec=pltpu.PrefetchScalarGridSpec(
            num_scalar_prefetch=3,
            grid=(1,),
            in_specs=[full(amps.shape[0]), full(fetched.shape[0])],
            out_specs=full(half),
            scratch_shapes=[pltpu.VMEM((half + 1, size, size), jnp.float32)],
        ),
        out_shape=jax.ShapeDtypeStruct((half, size, size), jnp.float32),
        compiler_params=pltpu.CompilerParams(vmem_limit_bytes=16 << 20),
        cost_estimate=pl.CostEstimate(
            flops=1 << 32, bytes_accessed=4 << 20, transcendentals=0
        ),
        name="contract_%d" % which,
    )(*tables, amps, fetched)


def encode_kernel(own, other, out):
    size = own.shape[1]
    for i in range(own.shape[0]):
        v = own[i] + other[i]
        top = jnp.max(jnp.abs(v), axis=0, keepdims=True)
        scale = jnp.ceil(jnp.log2(jnp.maximum(top, 1e-32)) * STEPS + 0.01)
        codes = v * (jnp.exp2(scale * (-1.0 / STEPS)) * TOP)
        out[i, :size] = jnp.floor(codes + 0.5).astype(jnp.int32).astype(jnp.int16)
        row = jnp.broadcast_to(scale, (out.shape[1] - size, size))
        out[i, size:] = row.astype(jnp.int32).astype(jnp.int16)


def encode(own, other):
    tiles, size, _ = own.shape
    return pl.pallas_call(
        encode_kernel,
        out_shape=jax.ShapeDtypeStruct((tiles, size + 16, size), jnp.int16),
        compiler_params=pltpu.CompilerParams(vmem_limit_bytes=16 << 20),
        cost_estimate=pl.CostEstimate(flops=1 << 20, bytes_accessed=3 << 20, transcendentals=0),
        name="encode",
    )(own, other)


def decode_kernel(pieces, out):
    size = out.shape[1]
    total = jnp.zeros((size, size), jnp.float32)
    for i in range(pieces.shape[0]):
        scale = pieces[i, size:].astype(jnp.int32).astype(jnp.float32)[:1]
        codes = pieces[i, :size].astype(jnp.int32).astype(jnp.float32)
        total += codes * (jnp.exp2(scale * (1.0 / STEPS)) * (1.0 / TOP))
    out[0] = total


def decode(pieces):
    size = pieces.shape[2]
    return pl.pallas_call(
        decode_kernel,
        out_shape=jax.ShapeDtypeStruct((1, size, size), jnp.float32),
        compiler_params=pltpu.CompilerParams(vmem_limit_bytes=4 << 20),
        cost_estimate=pl.CostEstimate(flops=1 << 20, bytes_accessed=1 << 20, transcendentals=0),
        name="decode",
    )(pieces)


def per_device(amplitudes, integrals, tasks, requests, counts):
    tile = amplitudes.shape[1]
    half = lax.axis_size("z")
    asked = jnp.clip(requests, 0, integrals.shape[0] - 1)
    wanted = lax.all_to_all(asked, "group", split_axis=0, concat_axis=0, tiled=True).reshape(-1)
    tables = task_tables(tasks, counts, lax.axis_index("core"), 2 * half)
    amps = jnp.concatenate([amplitudes, jnp.zeros((1, tile, tile), amplitudes.dtype)])
    wanted, tables, amps = lax.optimization_barrier((wanted, tables, amps))
    fetched = lax.all_to_all(
        select(wanted, integrals), "group", split_axis=0, concat_axis=0, tiled=True
    )
    other = contract(0, tables, amps, fetched, half)
    other = lax.ppermute(other, "core", [(0, 1), (1, 0)])
    own = contract(1, tables, amps, fetched, half)
    pieces = lax.all_to_all(encode(own, other), "z", split_axis=0, concat_axis=0, tiled=True)
    return decode(pieces)


def solution(mesh):
    finer = Mesh(mesh.devices.reshape(mesh.shape["group"], 16, 2), GROUP_MEMBER)
    placed = (
        P(GROUP_MEMBER, None, None),
        P(GROUP_MEMBER, None, None),
        P(GROUP_MEMBER, None),
        P(GROUP_MEMBER, None),
        P(GROUP_MEMBER),
    )
    return jax.shard_map(
        per_device,
        mesh=finer,
        in_specs=placed,
        out_specs=P(GROUP_MEMBER, None, None),
        check_vma=False,
    )
```

```python
import functools

import jax
import jax.numpy as jnp
from jax import lax
from jax.experimental import pallas as pl
from jax.experimental.pallas import tpu as pltpu
from jax.sharding import Mesh
from jax.sharding import PartitionSpec as P

GROUP_MEMBER = ("group", "zh", "zl", "core")
Z = ("zh", "zl")
PAIR = 2
UNROLL = 8
SLOTS = 512
TOP = 32760.0
SCALE_ROWS = 8
STEPS = 128.0


def select_kernel(base, wanted, local, out):
    rows, _, cap = wanted.shape
    for i in range(rows):
        for c in range(cap):
            out[i * cap + c] = local[base + wanted[i, 0, c]]


def select(wanted, local, base):
    size = local.shape[1]
    slots = wanted.shape[0] * wanted.shape[2]
    full = lambda n: pl.BlockSpec((n, size, size), lambda i, *_: (0, 0, 0))
    return pl.pallas_call(
        functools.partial(select_kernel, base),
        grid_spec=pltpu.PrefetchScalarGridSpec(
            num_scalar_prefetch=1,
            grid=(1,),
            in_specs=[full(local.shape[0])],
            out_specs=full(slots),
        ),
        out_shape=jax.ShapeDtypeStruct((slots, size, size), local.dtype),
        compiler_params=pltpu.CompilerParams(vmem_limit_bytes=16 << 20),
        cost_estimate=pl.CostEstimate(flops=0, bytes_accessed=2 << 20, transcendentals=0),
        name="select",
    )(wanted, local)


def task_tables(tasks, counts, core, parity, tiles, blank):
    a, s, r = tasks.T
    half = tiles // 2
    k = jnp.arange(tasks.shape[0], dtype=jnp.int32)
    valid = k < counts[0]
    side = ((r & 1) ^ core ^ 1) * half + (((r >> 1) & 1) ^ parity ^ 1) * (half // 2) + (r >> 2)
    q = jnp.where(valid, side, tiles)
    code = a + s * 32
    rank = jnp.sum(((q[:, None] == q[None, :]) & (k[None, :] < k[:, None])).astype(jnp.int32), 1)
    b = jnp.arange(tiles, dtype=jnp.int32)
    hot = q[:, None] == b[None, :]
    groups = (jnp.sum(hot.astype(jnp.int32), 0) + PAIR - 1) // PAIR
    ends = jnp.sum(jnp.where(b[:, None] <= b[None, :], groups[:, None], 0), 0)
    first = jnp.sum(jnp.where(hot, (ends - groups)[None, :], 0), 1)
    place = jnp.where(valid, first * PAIR + rank, -1)
    p = jnp.arange(SLOTS, dtype=jnp.int32)
    table = blank + jnp.sum(jnp.where(place[:, None] == p[None, :], code[:, None] - blank, 0), 0)
    j = jnp.arange(SLOTS // PAIR, dtype=jnp.int32)
    target = jnp.sum((ends[:, None] <= j[None, :]).astype(jnp.int32), 0)
    return table, target, ends


def contract_kernel(which, half, table, target, ends, amps, fetched, out, acc):
    low = ends[half - 1] if which else 0
    high = ends[which * half + half - 1]
    acc[...] = jnp.zeros_like(acc)

    def step(i, carry):
        products = []
        for u in range(UNROLL):
            j = low + i * UNROLL + u
            codes = [table[j * PAIR + n] for n in range(PAIR)]
            left = jnp.concatenate([amps[c & 31] for c in codes], axis=1)
            right = jnp.concatenate([fetched[c >> 5] for c in codes], axis=0)
            products.append(jnp.dot(left, right, preferred_element_type=jnp.float32))
        for u in range(UNROLL):
            j = low + i * UNROLL + u
            tile = jnp.where(j < high, target[j] - which * half, half)
            acc[tile] += products[u]
        return carry

    lax.fori_loop(0, (high - low + UNROLL - 1) // UNROLL, step, 0)
    out[...] = acc[:half]


def contract(which, tables, amps, fetched, half):
    size = amps.shape[1]
    full = lambda n: pl.BlockSpec((n, size, size), lambda i, *_: (0, 0, 0))
    return pl.pallas_call(
        functools.partial(contract_kernel, which, half),
        grid_spec=pltpu.PrefetchScalarGridSpec(
            num_scalar_prefetch=3,
            grid=(1,),
            in_specs=[full(amps.shape[0]), full(fetched.shape[0])],
            out_specs=full(half),
            scratch_shapes=[pltpu.VMEM((half + 1, size, size), jnp.float32)],
        ),
        out_shape=jax.ShapeDtypeStruct((half, size, size), jnp.float32),
        compiler_params=pltpu.CompilerParams(vmem_limit_bytes=16 << 20),
        cost_estimate=pl.CostEstimate(
            flops=1 << 32, bytes_accessed=4 << 20, transcendentals=0
        ),
        name="contract_%d" % which,
    )(*tables, amps, fetched)


def store_coded(v, out, i):
    rows = v.shape[0]
    top = jnp.max(jnp.abs(v), axis=0, keepdims=True)
    scale = jnp.ceil(jnp.log2(jnp.maximum(top, 1e-32)) * STEPS + 0.01)
    codes = v * (jnp.exp2(scale * (-1.0 / STEPS)) * TOP)
    out[i, :rows] = jnp.floor(codes + 0.5).astype(jnp.int32).astype(jnp.int16)
    row = jnp.broadcast_to(scale, (SCALE_ROWS, v.shape[1]))
    out[i, rows:] = row.astype(jnp.int32).astype(jnp.int16)


def load_coded(coded, i):
    rows = coded.shape[1] - SCALE_ROWS
    scale = coded[i, rows:].astype(jnp.int32).astype(jnp.float32)[:1]
    codes = coded[i, :rows].astype(jnp.int32).astype(jnp.float32)
    return codes * (jnp.exp2(scale * (1.0 / STEPS)) * (1.0 / TOP))


def plain_call(kernel, name, outs, *args):
    return pl.pallas_call(
        kernel,
        out_shape=outs,
        compiler_params=pltpu.CompilerParams(vmem_limit_bytes=8 << 20),
        cost_estimate=pl.CostEstimate(flops=1 << 20, bytes_accessed=2 << 20, transcendentals=0),
        name=name,
    )(*args)


def give_kernel(own, other, upper, lower):
    mid = own.shape[1] // 2
    for i in range(upper.shape[0]):
        store_coded(own[i, :mid] + other[i, :mid], upper, i)
        store_coded(own[i, mid:] + other[i, mid:], lower, i)


def take_kernel(own, other, upper, lower, out):
    for i in range(upper.shape[0]):
        k = upper.shape[0] + i
        more = jnp.concatenate([load_coded(upper, i), load_coded(lower, i)], axis=0)
        store_coded(own[k] + other[k] + more, out, i)


def finish_kernel(pieces, out):
    total = load_coded(pieces, 0)
    for i in range(1, pieces.shape[0]):
        total += load_coded(pieces, i)
    out[0] = total


def reduce_members(own, other):
    tiles, size, _ = own.shape
    coded = lambda rows: jax.ShapeDtypeStruct((tiles // 2, rows + SCALE_ROWS, size), jnp.int16)
    upper, lower = plain_call(give_kernel, "give", [coded(size // 2)] * 2, own, other)
    upper = lax.ppermute(upper, Z, [(z, z ^ 1) for z in range(tiles)])
    lower = lax.ppermute(lower, Z, [(z, (z + 1 if z % 2 else z - 1) % tiles) for z in range(tiles)])
    pieces = plain_call(take_kernel, "take", coded(size), own, other, upper, lower)
    pieces = lax.all_to_all(pieces, "zh", split_axis=0, concat_axis=0, tiled=True)
    return plain_call(
        finish_kernel, "finish", jax.ShapeDtypeStruct((1, size, size), jnp.float32), pieces
    )


def per_device(amplitudes, integrals, tasks, requests, counts):
    amount, tile, _ = amplitudes.shape
    half = lax.axis_size(Z)
    asked = requests.reshape(requests.shape[0], 1, requests.shape[1])
    wanted = lax.all_to_all(asked, "group", split_axis=0, concat_axis=0, tiled=True)
    core, parity = lax.axis_index("core"), lax.axis_index("zl")
    tables = task_tables(tasks, counts, core, parity, 2 * half, amount)
    blank = jnp.zeros((1, tile, tile), amplitudes.dtype)
    local = jnp.concatenate([amplitudes, blank, integrals])
    wanted, tables, local = lax.optimization_barrier((wanted, tables, local))
    fetched = lax.all_to_all(
        select(wanted, local, amount + 1), "group", split_axis=0, concat_axis=0, tiled=True
    )
    other = contract(0, tables, local, fetched, half)
    other = lax.ppermute(other, "core", [(0, 1), (1, 0)])
    own = contract(1, tables, local, fetched, half)
    return reduce_members(own, other)


def solution(mesh):
    finer = Mesh(mesh.devices.reshape(mesh.shape["group"], 8, 2, 2), GROUP_MEMBER)
    placed = (
        P(GROUP_MEMBER, None, None),
        P(GROUP_MEMBER, None, None),
        P(GROUP_MEMBER, None),
        P(GROUP_MEMBER, None),
        P(GROUP_MEMBER),
    )
    return jax.shard_map(
        per_device,
        mesh=finer,
        in_specs=placed,
        out_specs=P(GROUP_MEMBER, None, None),
        check_vma=False,
    )
```

```python
import functools

import jax
import jax.numpy as jnp
from jax import lax
from jax.experimental import pallas as pl
from jax.experimental.pallas import tpu as pltpu
from jax.sharding import Mesh
from jax.sharding import PartitionSpec as P

GROUP_MEMBER = ("group", "z", "core")
PAIR = 2
UNROLL = 8
SLOTS = 512
TOP = 32760.0
SCALE_ROWS = 8
SPLIT_LEVELS = 1
STEPS = 128.0


def select_kernel(base, wanted, local, out):
    rows, _, cap = wanted.shape
    for i in range(rows):
        for c in range(cap):
            out[i * cap + c] = local[base + wanted[i, 0, c]]


def select(wanted, local, base):
    size = local.shape[1]
    slots = wanted.shape[0] * wanted.shape[2]
    full = lambda n: pl.BlockSpec((n, size, size), lambda i, *_: (0, 0, 0))
    return pl.pallas_call(
        functools.partial(select_kernel, base),
        grid_spec=pltpu.PrefetchScalarGridSpec(
            num_scalar_prefetch=1,
            grid=(1,),
            in_specs=[full(local.shape[0])],
            out_specs=full(slots),
        ),
        out_shape=jax.ShapeDtypeStruct((slots, size, size), local.dtype),
        compiler_params=pltpu.CompilerParams(vmem_limit_bytes=16 << 20),
        cost_estimate=pl.CostEstimate(flops=0, bytes_accessed=2 << 20, transcendentals=0),
        name="select",
    )(wanted, local)


def task_tables(tasks, counts, core, tiles, blank):
    a, s, r = tasks.T
    half = tiles // 2
    k = jnp.arange(tasks.shape[0], dtype=jnp.int32)
    valid = k < counts[0]
    side = ((r & 1) ^ core ^ 1) * half + (r >> 1)
    q = jnp.where(valid, side, tiles)
    code = a + s * 32
    rank = jnp.sum(((q[:, None] == q[None, :]) & (k[None, :] < k[:, None])).astype(jnp.int32), 1)
    b = jnp.arange(tiles, dtype=jnp.int32)
    hot = q[:, None] == b[None, :]
    groups = (jnp.sum(hot.astype(jnp.int32), 0) + PAIR - 1) // PAIR
    ends = jnp.sum(jnp.where(b[:, None] <= b[None, :], groups[:, None], 0), 0)
    first = jnp.sum(jnp.where(hot, (ends - groups)[None, :], 0), 1)
    place = jnp.where(valid, first * PAIR + rank, -1)
    p = jnp.arange(SLOTS, dtype=jnp.int32)
    table = blank + jnp.sum(jnp.where(place[:, None] == p[None, :], code[:, None] - blank, 0), 0)
    j = jnp.arange(SLOTS // PAIR, dtype=jnp.int32)
    target = jnp.sum((ends[:, None] <= j[None, :]).astype(jnp.int32), 0)
    return table, target, ends


def contract_kernel(which, half, table, target, ends, amps, fetched, out, acc):
    low = ends[half - 1] if which else 0
    high = ends[which * half + half - 1]
    acc[...] = jnp.zeros_like(acc)

    def step(i, carry):
        products = []
        for u in range(UNROLL):
            j = low + i * UNROLL + u
            codes = [table[j * PAIR + n] for n in range(PAIR)]
            left = jnp.concatenate([amps[c & 31] for c in codes], axis=1)
            right = jnp.concatenate([fetched[c >> 5] for c in codes], axis=0)
            products.append(jnp.dot(left, right, preferred_element_type=jnp.float32))
        for u in range(UNROLL):
            j = low + i * UNROLL + u
            tile = jnp.where(j < high, target[j] - which * half, half)
            acc[tile] += products[u]
        return carry

    lax.fori_loop(0, (high - low + UNROLL - 1) // UNROLL, step, 0)
    out[...] = acc[:half]


def contract(which, tables, amps, fetched, half):
    size = amps.shape[1]
    full = lambda n: pl.BlockSpec((n, size, size), lambda i, *_: (0, 0, 0))
    return pl.pallas_call(
        functools.partial(contract_kernel, which, half),
        grid_spec=pltpu.PrefetchScalarGridSpec(
            num_scalar_prefetch=3,
            grid=(1,),
            in_specs=[full(amps.shape[0]), full(fetched.shape[0])],
            out_specs=full(half),
            scratch_shapes=[pltpu.VMEM((half + 1, size, size), jnp.float32)],
        ),
        out_shape=jax.ShapeDtypeStruct((half, size, size), jnp.float32),
        compiler_params=pltpu.CompilerParams(vmem_limit_bytes=16 << 20),
        cost_estimate=pl.CostEstimate(
            flops=1 << 32, bytes_accessed=4 << 20, transcendentals=0
        ),
        name="contract_%d" % which,
    )(*tables, amps, fetched)


def store_coded(v, out, i):
    rows = v.shape[0]
    top = jnp.max(jnp.abs(v), axis=0, keepdims=True)
    scale = jnp.ceil(jnp.log2(jnp.maximum(top, 1e-32)) * STEPS + 0.01)
    codes = v * (jnp.exp2(scale * (-1.0 / STEPS)) * TOP)
    out[i, :rows] = jnp.floor(codes + 0.5).astype(jnp.int32).astype(jnp.int16)
    row = jnp.broadcast_to(scale, (SCALE_ROWS, v.shape[1]))
    out[i, rows:] = row.astype(jnp.int32).astype(jnp.int16)


def load_coded(coded, i):
    rows = coded.shape[1] - SCALE_ROWS
    scale = coded[i, rows:].astype(jnp.int32).astype(jnp.float32)[:1]
    codes = coded[i, :rows].astype(jnp.int32).astype(jnp.float32)
    return codes * (jnp.exp2(scale * (1.0 / STEPS)) * (1.0 / TOP))


def fold_kernel(level, sources, inbox, z, *refs):
    held, arrived, (kept, *sent) = refs[:sources], refs[sources : sources + inbox], refs[sources + inbox :]
    bit = (z[0] >> level) & 1

    def tile(i):
        total = held[0][i]
        for more in held[1:]:
            total = total + more[i]
        if arrived:
            pieces = [load_coded(box, i) for box in arrived]
            total = total + (jnp.concatenate(pieces, axis=0) if len(pieces) > 1 else pieces[0])
        return total

    if not sent:
        kept[0] = tile(0)
        return
    for i in range(kept.shape[0]):
        kept[i] = tile(2 * i + bit)
        away = tile(2 * i + 1 - bit)
        rows = away.shape[0] // len(sent)
        for n, box in enumerate(sent):
            store_coded(away[n * rows : (n + 1) * rows], box, i)


def fold(level, z, held, arrived, tiles, size, parts):
    f32 = jax.ShapeDtypeStruct((max(tiles // 2, 1), size, size), jnp.float32)
    box = jax.ShapeDtypeStruct((tiles // 2, size // max(parts, 1) + SCALE_ROWS, size), jnp.int16)
    vmem = pl.BlockSpec()
    return pl.pallas_call(
        functools.partial(fold_kernel, level, len(held), len(arrived)),
        out_shape=[f32] + [box] * parts,
        in_specs=[pl.BlockSpec(memory_space=pltpu.SMEM)] + [vmem] * (len(held) + len(arrived)),
        compiler_params=pltpu.CompilerParams(vmem_limit_bytes=8 << 20),
        cost_estimate=pl.CostEstimate(flops=1 << 20, bytes_accessed=2 << 20, transcendentals=0),
        name="fold_%d" % level,
    )(z, *held, *arrived)


def reduce_members(own, other):
    tiles, size, _ = own.shape
    z = lax.axis_index("z").astype(jnp.int32).reshape(1)
    held, arrived, level = [own, other], [], 0
    count = tiles
    while count > 1:
        step = 1 << level
        near = [(i, i ^ step) for i in range(tiles)]
        far = [(i, (i + step if i & step else i - step) % tiles) for i in range(tiles)]
        routes = [near, far] if level < SPLIT_LEVELS else [near]
        kept, *boxes = fold(level, z, held, arrived, count, size, len(routes))
        held, arrived = [kept], [lax.ppermute(b, "z", r) for b, r in zip(boxes, routes)]
        level, count = level + 1, count // 2
    return fold(level, z, held, arrived, count, size, 0)[0]


def per_device(amplitudes, integrals, tasks, requests, counts):
    amount, tile, _ = amplitudes.shape
    half = lax.axis_size("z")
    asked = requests.reshape(requests.shape[0], 1, requests.shape[1])
    wanted = lax.all_to_all(asked, "group", split_axis=0, concat_axis=0, tiled=True)
    tables = task_tables(tasks, counts, lax.axis_index("core"), 2 * half, amount)
    blank = jnp.zeros((1, tile, tile), amplitudes.dtype)
    local = jnp.concatenate([amplitudes, blank, integrals])
    wanted, tables, local = lax.optimization_barrier((wanted, tables, local))
    fetched = lax.all_to_all(
        select(wanted, local, amount + 1), "group", split_axis=0, concat_axis=0, tiled=True
    )
    other = contract(0, tables, local, fetched, half)
    other = lax.ppermute(other, "core", [(0, 1), (1, 0)])
    own = contract(1, tables, local, fetched, half)
    return reduce_members(own, other)


def solution(mesh):
    finer = Mesh(mesh.devices.reshape(mesh.shape["group"], 16, 2), GROUP_MEMBER)
    placed = (
        P(GROUP_MEMBER, None, None),
        P(GROUP_MEMBER, None, None),
        P(GROUP_MEMBER, None),
        P(GROUP_MEMBER, None),
        P(GROUP_MEMBER),
    )
    return jax.shard_map(
        per_device,
        mesh=finer,
        in_specs=placed,
        out_specs=P(GROUP_MEMBER, None, None),
        check_vma=False,
    )
```

```python
import functools

import jax
import jax.numpy as jnp
from jax import lax
from jax.experimental import pallas as pl
from jax.experimental.pallas import tpu as pltpu
from jax.sharding import Mesh
from jax.sharding import PartitionSpec as P

GROUP_MEMBER = ("group", "zh", "zl", "core")
Z = ("zh", "zl")
PAIR = 2
UNROLL = 24
SLOTS = 512
TOP = 32760.0
SCALE_ROWS = 8
STEPS = 128.0


def select_kernel(base, wanted, local, out):
    rows, _, cap = wanted.shape
    for i in range(rows):
        for c in range(cap):
            out[i * cap + c] = local[base + wanted[i, 0, c]]


def select(wanted, local, base):
    size = local.shape[1]
    slots = wanted.shape[0] * wanted.shape[2]
    full = lambda n: pl.BlockSpec((n, size, size), lambda i, *_: (0, 0, 0))
    return pl.pallas_call(
        functools.partial(select_kernel, base),
        grid_spec=pltpu.PrefetchScalarGridSpec(
            num_scalar_prefetch=1,
            grid=(1,),
            in_specs=[full(local.shape[0])],
            out_specs=full(slots),
        ),
        out_shape=jax.ShapeDtypeStruct((slots, size, size), local.dtype),
        compiler_params=pltpu.CompilerParams(vmem_limit_bytes=16 << 20),
        cost_estimate=pl.CostEstimate(flops=0, bytes_accessed=2 << 20, transcendentals=0),
        name="select",
    )(wanted, local)


def task_tables(tasks, counts, core, parity, tiles, blank):
    a, s, r = tasks.T
    half = tiles // 2
    k = jnp.arange(tasks.shape[0], dtype=jnp.int32)
    valid = k < counts[0]
    side = ((r & 1) ^ core ^ 1) * half + (((r >> 1) & 1) ^ parity ^ 1) * (half // 2) + (r >> 2)
    q = jnp.where(valid, side, tiles)
    code = a + s * 32
    rank = jnp.sum(((q[:, None] == q[None, :]) & (k[None, :] < k[:, None])).astype(jnp.int32), 1)
    b = jnp.arange(tiles, dtype=jnp.int32)
    hot = q[:, None] == b[None, :]
    groups = (jnp.sum(hot.astype(jnp.int32), 0) + PAIR - 1) // PAIR
    ends = jnp.sum(jnp.where(b[:, None] <= b[None, :], groups[:, None], 0), 0)
    first = jnp.sum(jnp.where(hot, (ends - groups)[None, :], 0), 1)
    place = jnp.where(valid, first * PAIR + rank, -1)
    p = jnp.arange(SLOTS, dtype=jnp.int32)
    table = blank + jnp.sum(jnp.where(place[:, None] == p[None, :], code[:, None] - blank, 0), 0)
    j = jnp.arange(SLOTS // PAIR, dtype=jnp.int32)
    target = jnp.sum((ends[:, None] <= j[None, :]).astype(jnp.int32), 0)
    return table, target, ends


def contract_kernel(which, half, blank, table, target, ends, amps, fetched, out):
    low = ends[half - 1] if which else 0
    high = ends[which * half + half - 1]
    out[...] = jnp.zeros_like(out)

    def step(i, carry):
        products = []
        for u in range(UNROLL):
            j = low + i * UNROLL + u
            codes = [jnp.where(j < high, table[j * PAIR + n], blank) for n in range(PAIR)]
            left = jnp.concatenate([amps[c & 31] for c in codes], axis=1)
            right = jnp.concatenate([fetched[c >> 5] for c in codes], axis=0)
            products.append(jnp.dot(left, right, preferred_element_type=jnp.float32))
        for u in range(UNROLL):
            j = low + i * UNROLL + u
            out[jnp.minimum(target[j] - which * half, half - 1)] += products[u]
        return carry

    lax.fori_loop(0, (high - low + UNROLL - 1) // UNROLL, step, 0)


def contract(which, tables, amps, fetched, half, blank):
    size = amps.shape[1]
    full = lambda n: pl.BlockSpec((n, size, size), lambda i, *_: (0, 0, 0))
    return pl.pallas_call(
        functools.partial(contract_kernel, which, half, blank),
        grid_spec=pltpu.PrefetchScalarGridSpec(
            num_scalar_prefetch=3,
            grid=(1,),
            in_specs=[full(amps.shape[0]), full(fetched.shape[0])],
            out_specs=full(half),
        ),
        out_shape=jax.ShapeDtypeStruct((half, size, size), jnp.float32),
        compiler_params=pltpu.CompilerParams(vmem_limit_bytes=16 << 20),
        cost_estimate=pl.CostEstimate(
            flops=1 << 32, bytes_accessed=4 << 20, transcendentals=0
        ),
        name="contract_%d" % which,
    )(*tables, amps, fetched)


def store_coded(v, out, i):
    rows = v.shape[0]
    top = jnp.max(jnp.abs(v), axis=0, keepdims=True)
    scale = jnp.ceil(jnp.log2(jnp.maximum(top, 1e-32)) * STEPS + 0.01)
    codes = v * (jnp.exp2(scale * (-1.0 / STEPS)) * TOP)
    out[i, :rows] = jnp.floor(codes + 0.5).astype(jnp.int32).astype(jnp.int16)
    row = jnp.broadcast_to(scale, (SCALE_ROWS, v.shape[1]))
    out[i, rows:] = row.astype(jnp.int32).astype(jnp.int16)


def load_coded(coded, i):
    rows = coded.shape[1] - SCALE_ROWS
    scale = coded[i, rows:].astype(jnp.int32).astype(jnp.float32)[:1]
    codes = coded[i, :rows].astype(jnp.int32).astype(jnp.float32)
    return codes * (jnp.exp2(scale * (1.0 / STEPS)) * (1.0 / TOP))


def plain_call(kernel, name, outs, *args):
    return pl.pallas_call(
        kernel,
        out_shape=outs,
        compiler_params=pltpu.CompilerParams(vmem_limit_bytes=8 << 20),
        cost_estimate=pl.CostEstimate(flops=1 << 20, bytes_accessed=2 << 20, transcendentals=0),
        name=name,
    )(*args)


def give_kernel(own, other, out):
    for i in range(out.shape[0]):
        store_coded(own[i] + other[i], out, i)


def take_kernel(own, other, arrived, out):
    for i in range(out.shape[0]):
        k = out.shape[0] + i
        store_coded(own[k] + other[k] + load_coded(arrived, i), out, i)


def finish_kernel(pieces, out):
    total = load_coded(pieces, 0)
    for i in range(1, pieces.shape[0]):
        total += load_coded(pieces, i)
    out[0] = total


def reduce_members(own, other):
    tiles, size, _ = own.shape
    coded = jax.ShapeDtypeStruct((tiles // 2, size + SCALE_ROWS, size), jnp.int16)
    arrived = plain_call(give_kernel, "give", coded, own, other)
    arrived = lax.ppermute(arrived, "zl", [(0, 1), (1, 0)])
    pieces = plain_call(take_kernel, "take", coded, own, other, arrived)
    pieces = lax.all_to_all(pieces, "zh", split_axis=0, concat_axis=0, tiled=True)
    return plain_call(
        finish_kernel, "finish", jax.ShapeDtypeStruct((1, size, size), jnp.float32), pieces
    )


def per_device(amplitudes, integrals, tasks, requests, counts):
    amount, tile, _ = amplitudes.shape
    half = lax.axis_size(Z)
    asked = requests.reshape(requests.shape[0], 1, requests.shape[1])
    wanted = lax.all_to_all(asked, "group", split_axis=0, concat_axis=0, tiled=True)
    core, parity = lax.axis_index("core"), lax.axis_index("zl")
    tables = task_tables(tasks, counts, core, parity, 2 * half, amount)
    blank = jnp.zeros((1, tile, tile), amplitudes.dtype)
    local = jnp.concatenate([amplitudes, blank, integrals])
    wanted, tables, local = lax.optimization_barrier((wanted, tables, local))
    fetched = lax.all_to_all(
        select(wanted, local, amount + 1), "group", split_axis=0, concat_axis=0, tiled=True
    )
    other = contract(0, tables, local, fetched, half, amount)
    other = lax.ppermute(other, "core", [(0, 1), (1, 0)])
    own = contract(1, tables, local, fetched, half, amount)
    return reduce_members(own, other)


def solution(mesh):
    finer = Mesh(mesh.devices.reshape(mesh.shape["group"], 8, 2, 2), GROUP_MEMBER)
    placed = (
        P(GROUP_MEMBER, None, None),
        P(GROUP_MEMBER, None, None),
        P(GROUP_MEMBER, None),
        P(GROUP_MEMBER, None),
        P(GROUP_MEMBER),
    )
    return jax.shard_map(
        per_device,
        mesh=finer,
        in_specs=placed,
        out_specs=P(GROUP_MEMBER, None, None),
        check_vma=False,
    )
```

```python
import functools

import jax
import jax.numpy as jnp
from jax import lax
from jax.experimental import pallas as pl
from jax.experimental.pallas import tpu as pltpu
from jax.sharding import Mesh
from jax.sharding import PartitionSpec as P

GROUP_MEMBER = ("group", "zh", "zl", "core")
Z = ("zh", "zl")
PAIR = 2
UNROLL = 24
SLOTS = 512
TOP = 32760.0
SCALE_ROWS = 8
STEPS = 128.0


def select_kernel(base, wanted, local, out):
    rows, _, cap = wanted.shape
    for i in range(rows):
        for c in range(cap):
            out[i * cap + c] = local[base + wanted[i, 0, c]]


def select(wanted, local, base):
    size = local.shape[1]
    slots = wanted.shape[0] * wanted.shape[2]
    full = lambda n: pl.BlockSpec((n, size, size), lambda i, *_: (0, 0, 0))
    return pl.pallas_call(
        functools.partial(select_kernel, base),
        grid_spec=pltpu.PrefetchScalarGridSpec(
            num_scalar_prefetch=1,
            grid=(1,),
            in_specs=[full(local.shape[0])],
            out_specs=full(slots),
        ),
        out_shape=jax.ShapeDtypeStruct((slots, size, size), local.dtype),
        compiler_params=pltpu.CompilerParams(vmem_limit_bytes=16 << 20),
        cost_estimate=pl.CostEstimate(flops=0, bytes_accessed=2 << 20, transcendentals=0),
        name="select",
    )(wanted, local)


def task_tables(tasks, counts, core, parity, tiles, blank):
    a, s, r = tasks.T
    half = tiles // 2
    k = jnp.arange(tasks.shape[0], dtype=jnp.int32)
    valid = k < counts[0]
    side = ((r & 1) ^ core ^ 1) * half + (((r >> 1) & 1) ^ parity ^ 1) * (half // 2) + (r >> 2)
    q = jnp.where(valid, side, tiles)
    code = a + s * 32
    rank = jnp.sum(((q[:, None] == q[None, :]) & (k[None, :] < k[:, None])).astype(jnp.int32), 1)
    b = jnp.arange(tiles, dtype=jnp.int32)
    hot = q[:, None] == b[None, :]
    groups = (jnp.sum(hot.astype(jnp.int32), 0) + PAIR - 1) // PAIR
    ends = jnp.sum(jnp.where(b[:, None] <= b[None, :], groups[:, None], 0), 0)
    first = jnp.sum(jnp.where(hot, (ends - groups)[None, :], 0), 1)
    place = jnp.where(valid, first * PAIR + rank, -1)
    p = jnp.arange(SLOTS, dtype=jnp.int32)
    table = blank + jnp.sum(jnp.where(place[:, None] == p[None, :], code[:, None] - blank, 0), 0)
    j = jnp.arange(SLOTS // PAIR, dtype=jnp.int32)
    target = jnp.sum((ends[:, None] <= j[None, :]).astype(jnp.int32), 0)
    return table, target, ends


def contract_kernel(which, half, blank, table, target, ends, amps, fetched, out):
    low = ends[half - 1] if which else 0
    high = ends[which * half + half - 1]
    out[...] = jnp.zeros_like(out)

    def step(i, carry):
        products = []
        for u in range(UNROLL):
            j = low + i * UNROLL + u
            codes = [jnp.where(j < high, table[j * PAIR + n], blank) for n in range(PAIR)]
            left = jnp.concatenate([amps[c & 31] for c in codes], axis=1)
            right = jnp.concatenate([fetched[c >> 5] for c in codes], axis=0)
            products.append(jnp.dot(left, right, preferred_element_type=jnp.float32))
        for u in range(UNROLL):
            j = low + i * UNROLL + u
            out[jnp.minimum(target[j] - which * half, half - 1)] += products[u]
        return carry

    lax.fori_loop(0, (high - low + UNROLL - 1) // UNROLL, step, 0)


def contract(which, tables, amps, fetched, half, blank):
    size = amps.shape[1]
    full = lambda n: pl.BlockSpec((n, size, size), lambda i, *_: (0, 0, 0))
    return pl.pallas_call(
        functools.partial(contract_kernel, which, half, blank),
        grid_spec=pltpu.PrefetchScalarGridSpec(
            num_scalar_prefetch=3,
            grid=(1,),
            in_specs=[full(amps.shape[0]), full(fetched.shape[0])],
            out_specs=full(half),
        ),
        out_shape=jax.ShapeDtypeStruct((half, size, size), jnp.float32),
        compiler_params=pltpu.CompilerParams(vmem_limit_bytes=16 << 20),
        cost_estimate=pl.CostEstimate(
            flops=1 << 32, bytes_accessed=4 << 20, transcendentals=0
        ),
        name="contract_%d" % which,
    )(*tables, amps, fetched)


def store_coded(v, out, i):
    rows = v.shape[0]
    top = jnp.max(jnp.abs(v), axis=0, keepdims=True)
    scale = jnp.ceil(jnp.log2(jnp.maximum(top, 1e-32)) * STEPS + 0.01)
    codes = v * (jnp.exp2(scale * (-1.0 / STEPS)) * TOP)
    out[i, :rows] = jnp.floor(codes + 0.5).astype(jnp.int32).astype(jnp.int16)
    row = jnp.broadcast_to(scale, (SCALE_ROWS, v.shape[1]))
    out[i, rows:] = row.astype(jnp.int32).astype(jnp.int16)


def load_coded(coded, i):
    rows = coded.shape[1] - SCALE_ROWS
    scale = coded[i, rows:].astype(jnp.int32).astype(jnp.float32)[:1]
    codes = coded[i, :rows].astype(jnp.int32).astype(jnp.float32)
    return codes * (jnp.exp2(scale * (1.0 / STEPS)) * (1.0 / TOP))


def plain_call(kernel, name, outs, *args):
    return pl.pallas_call(
        kernel,
        out_shape=outs,
        compiler_params=pltpu.CompilerParams(vmem_limit_bytes=8 << 20),
        cost_estimate=pl.CostEstimate(flops=1 << 20, bytes_accessed=2 << 20, transcendentals=0),
        name=name,
    )(*args)


def give_kernel(own, other, out):
    for i in range(out.shape[0]):
        store_coded(own[i] + other[i], out, i)


def take_kernel(own, other, arrived, out):
    for i in range(out.shape[0]):
        k = out.shape[0] + i
        store_coded(own[k] + other[k] + load_coded(arrived, i), out, i)


def finish_kernel(pieces, out):
    total = load_coded(pieces, 0)
    for i in range(1, pieces.shape[0]):
        total += load_coded(pieces, i)
    out[0] = total


def reduce_members(own, other):
    tiles, size, _ = own.shape
    coded = jax.ShapeDtypeStruct((tiles // 2, size + SCALE_ROWS, size), jnp.int16)
    arrived = plain_call(give_kernel, "give", coded, own, other)
    route = []
    for z in range(tiles):
        route.append((2 * z, 2 * (z ^ 1)))
        route.append((2 * z + 1, 2 * ((z + 1 if z % 2 else z - 1) % tiles) + 1))
    arrived = lax.ppermute(arrived, (*Z, "core"), route)
    pieces = plain_call(take_kernel, "take", coded, own, other, arrived)
    pieces = lax.all_to_all(pieces, "zh", split_axis=0, concat_axis=0, tiled=True)
    return plain_call(
        finish_kernel, "finish", jax.ShapeDtypeStruct((1, size, size), jnp.float32), pieces
    )


def per_device(amplitudes, integrals, tasks, requests, counts):
    amount, tile, _ = amplitudes.shape
    half = lax.axis_size(Z)
    asked = requests.reshape(requests.shape[0], 1, requests.shape[1])
    wanted = lax.all_to_all(asked, "group", split_axis=0, concat_axis=0, tiled=True)
    core, parity = lax.axis_index("core"), lax.axis_index("zl")
    tables = task_tables(tasks, counts, core, parity, 2 * half, amount)
    blank = jnp.zeros((1, tile, tile), amplitudes.dtype)
    local = jnp.concatenate([amplitudes, blank, integrals])
    wanted, tables, local = lax.optimization_barrier((wanted, tables, local))
    fetched = lax.all_to_all(
        select(wanted, local, amount + 1), "group", split_axis=0, concat_axis=0, tiled=True
    )
    other = contract(0, tables, local, fetched, half, amount)
    other = lax.ppermute(other, "core", [(0, 1), (1, 0)])
    own = contract(1, tables, local, fetched, half, amount)
    return reduce_members(own, other)


def solution(mesh):
    finer = Mesh(mesh.devices.reshape(mesh.shape["group"], 8, 2, 2), GROUP_MEMBER)
    placed = (
        P(GROUP_MEMBER, None, None),
        P(GROUP_MEMBER, None, None),
        P(GROUP_MEMBER, None),
        P(GROUP_MEMBER, None),
        P(GROUP_MEMBER),
    )
    return jax.shard_map(
        per_device,
        mesh=finer,
        in_specs=placed,
        out_specs=P(GROUP_MEMBER, None, None),
        check_vma=False,
    )
```

```python
import functools

import jax
import jax.numpy as jnp
from jax import lax
from jax.experimental import pallas as pl
from jax.experimental.pallas import tpu as pltpu
from jax.sharding import Mesh
from jax.sharding import PartitionSpec as P

GROUP_MEMBER = ("group", "zh", "zl", "core")
Z = ("zh", "zl")
PAIR = 2
UNROLL = 16
SLOTS = 512
TOP = 32760.0
SCALE_ROWS = 8
STEPS = 128.0


def select_kernel(base, wanted, local, out):
    rows, _, cap = wanted.shape
    for i in range(rows):
        for c in range(cap):
            out[i * cap + c] = local[base + wanted[i, 0, c]]


def select(wanted, local, base):
    size = local.shape[1]
    slots = wanted.shape[0] * wanted.shape[2]
    full = lambda n: pl.BlockSpec((n, size, size), lambda i, *_: (0, 0, 0))
    return pl.pallas_call(
        functools.partial(select_kernel, base),
        grid_spec=pltpu.PrefetchScalarGridSpec(
            num_scalar_prefetch=1,
            grid=(1,),
            in_specs=[full(local.shape[0])],
            out_specs=full(slots),
        ),
        out_shape=jax.ShapeDtypeStruct((slots, size, size), local.dtype),
        compiler_params=pltpu.CompilerParams(vmem_limit_bytes=16 << 20),
        cost_estimate=pl.CostEstimate(flops=0, bytes_accessed=2 << 20, transcendentals=0),
        name="select",
    )(wanted, local)


def task_tables(tasks, counts, core, parity, tiles, blank):
    a, s, r = tasks.T
    half = tiles // 2
    k = jnp.arange(tasks.shape[0], dtype=jnp.int32)
    valid = k < counts[0]
    side = (((r >> 1) & 1) ^ parity ^ 1) * half + ((r & 1) ^ core ^ 1) * (half // 2) + (r >> 2)
    q = jnp.where(valid, side, tiles)
    code = a + s * 32
    rank = jnp.sum(((q[:, None] == q[None, :]) & (k[None, :] < k[:, None])).astype(jnp.int32), 1)
    b = jnp.arange(tiles, dtype=jnp.int32)
    hot = q[:, None] == b[None, :]
    groups = (jnp.sum(hot.astype(jnp.int32), 0) + PAIR - 1) // PAIR
    ends = jnp.sum(jnp.where(b[:, None] <= b[None, :], groups[:, None], 0), 0)
    first = jnp.sum(jnp.where(hot, (ends - groups)[None, :], 0), 1)
    place = jnp.where(valid, first * PAIR + rank, -1)
    p = jnp.arange(SLOTS, dtype=jnp.int32)
    table = blank + jnp.sum(jnp.where(place[:, None] == p[None, :], code[:, None] - blank, 0), 0)
    j = jnp.arange(SLOTS // PAIR, dtype=jnp.int32)
    target = jnp.sum((ends[:, None] <= j[None, :]).astype(jnp.int32), 0)
    return table, target, ends


def contract_kernel(which, part, blank, table, target, ends, amps, fetched, out):
    low = ends[which * part - 1] if which else 0
    high = ends[which * part + part - 1]
    out[...] = jnp.zeros_like(out)

    def step(i, carry):
        products = []
        for u in range(UNROLL):
            j = low + i * UNROLL + u
            codes = [jnp.where(j < high, table[j * PAIR + n], blank) for n in range(PAIR)]
            left = jnp.concatenate([amps[c & 31] for c in codes], axis=1)
            right = jnp.concatenate([fetched[c >> 5] for c in codes], axis=0)
            products.append(jnp.dot(left, right, preferred_element_type=jnp.float32))
        for u in range(UNROLL):
            j = low + i * UNROLL + u
            out[jnp.minimum(target[j] - which * part, part - 1)] += products[u]
        return carry

    lax.fori_loop(0, (high - low + UNROLL - 1) // UNROLL, step, 0)


def contract(which, tables, amps, fetched, part, blank):
    size = amps.shape[1]
    full = lambda n: pl.BlockSpec((n, size, size), lambda i, *_: (0, 0, 0))
    return pl.pallas_call(
        functools.partial(contract_kernel, which, part, blank),
        grid_spec=pltpu.PrefetchScalarGridSpec(
            num_scalar_prefetch=3,
            grid=(1,),
            in_specs=[full(amps.shape[0]), full(fetched.shape[0])],
            out_specs=full(part),
        ),
        out_shape=jax.ShapeDtypeStruct((part, size, size), jnp.float32),
        compiler_params=pltpu.CompilerParams(vmem_limit_bytes=16 << 20),
        cost_estimate=pl.CostEstimate(
            flops=1 << 31, bytes_accessed=3 << 20, transcendentals=0
        ),
        name="contract_%d" % which,
    )(*tables, amps, fetched)


def store_coded(v, out, i):
    rows = v.shape[0]
    top = jnp.max(jnp.abs(v), axis=0, keepdims=True)
    scale = jnp.ceil(jnp.log2(jnp.maximum(top, 1e-32)) * STEPS + 0.01)
    codes = v * (jnp.exp2(scale * (-1.0 / STEPS)) * TOP)
    out[i, :rows] = jnp.floor(codes + 0.5).astype(jnp.int32).astype(jnp.int16)
    row = jnp.broadcast_to(scale, (SCALE_ROWS, v.shape[1]))
    out[i, rows:] = row.astype(jnp.int32).astype(jnp.int16)


def load_coded(coded, i):
    rows = coded.shape[1] - SCALE_ROWS
    scale = coded[i, rows:].astype(jnp.int32).astype(jnp.float32)[:1]
    codes = coded[i, :rows].astype(jnp.int32).astype(jnp.float32)
    return codes * (jnp.exp2(scale * (1.0 / STEPS)) * (1.0 / TOP))


def plain_call(kernel, name, outs, *args):
    return pl.pallas_call(
        kernel,
        out_shape=outs,
        compiler_params=pltpu.CompilerParams(vmem_limit_bytes=8 << 20),
        cost_estimate=pl.CostEstimate(flops=1 << 20, bytes_accessed=2 << 20, transcendentals=0),
        name=name,
    )(*args)


def give_kernel(own, other, out):
    for i in range(out.shape[0]):
        store_coded(own[i] + other[i], out, i)


def take_kernel(own, other, arrived, out):
    for i in range(out.shape[0]):
        store_coded(own[i] + other[i] + load_coded(arrived, i), out, i)


def finish_kernel(pieces, out):
    total = load_coded(pieces, 0)
    for i in range(1, pieces.shape[0]):
        total += load_coded(pieces, i)
    out[0] = total


def near_route(chips):
    route = []
    for z in range(chips):
        route.append((2 * z, 2 * (z ^ 1)))
        route.append((2 * z + 1, 2 * ((z + 1 if z % 2 else z - 1) % chips) + 1))
    return route


def per_device(amplitudes, integrals, tasks, requests, counts):
    amount, tile, _ = amplitudes.shape
    half = lax.axis_size(Z)
    asked = requests.reshape(requests.shape[0], 1, requests.shape[1])
    wanted = lax.all_to_all(asked, "group", split_axis=0, concat_axis=0, tiled=True)
    core, parity = lax.axis_index("core"), lax.axis_index("zl")
    tables = task_tables(tasks, counts, core, parity, 2 * half, amount)
    blank = jnp.zeros((1, tile, tile), amplitudes.dtype)
    local = jnp.concatenate([amplitudes, blank, integrals])
    wanted, tables, local = lax.optimization_barrier((wanted, tables, local))
    fetched = lax.all_to_all(
        select(wanted, local, amount + 1), "group", split_axis=0, concat_axis=0, tiled=True
    )
    part = half // 2
    tiles = lambda which, tables: contract(which, tables, local, fetched, part, amount)
    swap = lambda x: lax.ppermute(x, "core", [(0, 1), (1, 0)])
    coded = jax.ShapeDtypeStruct((part, tile + SCALE_ROWS, tile), jnp.int16)

    other = swap(tiles(0, tables))
    away = plain_call(give_kernel, "give", coded, tiles(1, tables), other)
    away, tables = lax.optimization_barrier((away, tables))
    arrived = lax.ppermute(away, (*Z, "core"), near_route(half))
    other = swap(tiles(2, tables))
    pieces = plain_call(take_kernel, "take", coded, tiles(3, tables), other, arrived)
    pieces = lax.all_to_all(pieces, "zh", split_axis=0, concat_axis=0, tiled=True)
    total = jax.ShapeDtypeStruct((1, tile, tile), jnp.float32)
    return plain_call(finish_kernel, "finish", total, pieces)


def solution(mesh):
    finer = Mesh(mesh.devices.reshape(mesh.shape["group"], 8, 2, 2), GROUP_MEMBER)
    placed = (
        P(GROUP_MEMBER, None, None),
        P(GROUP_MEMBER, None, None),
        P(GROUP_MEMBER, None),
        P(GROUP_MEMBER, None),
        P(GROUP_MEMBER),
    )
    return jax.shard_map(
        per_device,
        mesh=finer,
        in_specs=placed,
        out_specs=P(GROUP_MEMBER, None, None),
        check_vma=False,
    )
```

```python
import functools

import jax
import jax.numpy as jnp
from jax import lax
from jax.experimental import pallas as pl
from jax.experimental.pallas import tpu as pltpu
from jax.sharding import Mesh
from jax.sharding import PartitionSpec as P

GROUP_MEMBER = ("group", "zh", "zl", "core")
Z = ("zh", "zl")
PAIR = 2
UNROLL = 24
SLOTS = 512
TOP = 32760.0
SCALE_ROWS = 8
STEPS = 128.0


def select_kernel(base, wanted, local, out):
    rows, _, cap = wanted.shape
    for i in range(rows):
        for c in range(cap):
            out[i * cap + c] = local[base + wanted[i, 0, c]]


def select(wanted, local, base):
    size = local.shape[1]
    slots = wanted.shape[0] * wanted.shape[2]
    full = lambda n: pl.BlockSpec((n, size, size), lambda i, *_: (0, 0, 0))
    return pl.pallas_call(
        functools.partial(select_kernel, base),
        grid_spec=pltpu.PrefetchScalarGridSpec(
            num_scalar_prefetch=1,
            grid=(1,),
            in_specs=[full(local.shape[0])],
            out_specs=full(slots),
        ),
        out_shape=jax.ShapeDtypeStruct((slots, size, size), local.dtype),
        compiler_params=pltpu.CompilerParams(vmem_limit_bytes=16 << 20),
        cost_estimate=pl.CostEstimate(flops=0, bytes_accessed=2 << 20, transcendentals=0),
        name="select",
    )(wanted, local)


def task_tables(tasks, counts, core, parity, tiles, blank):
    a, s, r = tasks.T
    half = tiles // 2
    k = jnp.arange(tasks.shape[0], dtype=jnp.int32)
    valid = k < counts[0]
    side = ((r & 1) ^ core ^ 1) * half + (((r >> 1) & 1) ^ parity ^ 1) * (half // 2) + (r >> 2)
    q = jnp.where(valid, side, tiles)
    code = a + s * 32
    rank = jnp.sum(((q[:, None] == q[None, :]) & (k[None, :] < k[:, None])).astype(jnp.int32), 1)
    b = jnp.arange(tiles, dtype=jnp.int32)
    hot = q[:, None] == b[None, :]
    groups = (jnp.sum(hot.astype(jnp.int32), 0) + PAIR - 1) // PAIR
    ends = jnp.sum(jnp.where(b[:, None] <= b[None, :], groups[:, None], 0), 0)
    first = jnp.sum(jnp.where(hot, (ends - groups)[None, :], 0), 1)
    place = jnp.where(valid, first * PAIR + rank, -1)
    p = jnp.arange(SLOTS, dtype=jnp.int32)
    table = blank + jnp.sum(jnp.where(place[:, None] == p[None, :], code[:, None] - blank, 0), 0)
    j = jnp.arange(SLOTS // PAIR, dtype=jnp.int32)
    target = jnp.sum((ends[:, None] <= j[None, :]).astype(jnp.int32), 0)
    return table, target, ends


def contract_kernel(which, half, blank, table, target, ends, amps, fetched, out):
    low = ends[half - 1] if which else 0
    high = ends[which * half + half - 1]
    out[...] = jnp.zeros_like(out)

    def step(i, carry):
        products = []
        for u in range(UNROLL):
            j = low + i * UNROLL + u
            codes = [jnp.where(j < high, table[j * PAIR + n], blank) for n in range(PAIR)]
            left = jnp.concatenate([amps[c & 31] for c in codes], axis=1)
            right = jnp.concatenate([fetched[c >> 5] for c in codes], axis=0)
            products.append(jnp.dot(left, right, preferred_element_type=jnp.float32))
        for u in range(UNROLL):
            j = low + i * UNROLL + u
            out[jnp.minimum(target[j] - which * half, half - 1)] += products[u]
        return carry

    lax.fori_loop(0, (high - low + UNROLL - 1) // UNROLL, step, 0)


def contract(which, tables, amps, fetched, half, blank):
    size = amps.shape[1]
    full = lambda n: pl.BlockSpec((n, size, size), lambda i, *_: (0, 0, 0))
    return pl.pallas_call(
        functools.partial(contract_kernel, which, half, blank),
        grid_spec=pltpu.PrefetchScalarGridSpec(
            num_scalar_prefetch=3,
            grid=(1,),
            in_specs=[full(amps.shape[0]), full(fetched.shape[0])],
            out_specs=full(half),
        ),
        out_shape=jax.ShapeDtypeStruct((half, size, size), jnp.float32),
        compiler_params=pltpu.CompilerParams(vmem_limit_bytes=16 << 20),
        cost_estimate=pl.CostEstimate(
            flops=1 << 32, bytes_accessed=4 << 20, transcendentals=0
        ),
        name="contract_%d" % which,
    )(*tables, amps, fetched)


def store_coded(v, out, i):
    rows = v.shape[0]
    top = jnp.max(jnp.abs(v), axis=0, keepdims=True)
    scale = jnp.ceil(jnp.log2(jnp.maximum(top, 1e-32)) * STEPS + 0.01)
    codes = v * (jnp.exp2(scale * (-1.0 / STEPS)) * TOP)
    out[i, :rows] = jnp.floor(codes + 0.5).astype(jnp.int32).astype(jnp.int16)
    row = jnp.broadcast_to(scale, (SCALE_ROWS, v.shape[1]))
    out[i, rows:] = row.astype(jnp.int32).astype(jnp.int16)


def load_coded(coded, i):
    rows = coded.shape[1] - SCALE_ROWS
    scale = coded[i, rows:].astype(jnp.int32).astype(jnp.float32)[:1]
    codes = coded[i, :rows].astype(jnp.int32).astype(jnp.float32)
    return codes * (jnp.exp2(scale * (1.0 / STEPS)) * (1.0 / TOP))


def plain_call(kernel, name, outs, *args):
    return pl.pallas_call(
        kernel,
        out_shape=outs,
        compiler_params=pltpu.CompilerParams(vmem_limit_bytes=8 << 20),
        cost_estimate=pl.CostEstimate(flops=1 << 20, bytes_accessed=2 << 20, transcendentals=0),
        name=name,
    )(*args)


def give_kernel(own, other, out):
    for i in range(out.shape[0]):
        store_coded(own[i] + other[i], out, i)


def take_kernel(own, other, arrived, out):
    for i in range(out.shape[0]):
        k = out.shape[0] + i
        store_coded(own[k] + other[k] + load_coded(arrived, i), out, i)


def finish_kernel(pieces, out):
    total = load_coded(pieces, 0)
    for i in range(1, pieces.shape[0]):
        total += load_coded(pieces, i)
    out[0] = total


def reduce_members(own, other):
    tiles, size, _ = own.shape
    coded = jax.ShapeDtypeStruct((tiles // 2, size + SCALE_ROWS, size), jnp.int16)
    arrived = plain_call(give_kernel, "give", coded, own, other)
    route = []
    for z in range(tiles):
        route.append((2 * z, 2 * (z ^ 1)))
        route.append((2 * z + 1, 2 * ((z + 1 if z % 2 else z - 1) % tiles) + 1))
    arrived = lax.ppermute(arrived, (*Z, "core"), route)
    pieces = plain_call(take_kernel, "take", coded, own, other, arrived)
    pieces = lax.all_to_all(pieces, "zh", split_axis=0, concat_axis=0, tiled=True)
    return plain_call(
        finish_kernel, "finish", jax.ShapeDtypeStruct((1, size, size), jnp.float32), pieces
    )


def per_device(amplitudes, integrals, tasks, requests, counts):
    amount, tile, _ = amplitudes.shape
    half = lax.axis_size(Z)
    asked = requests.reshape(requests.shape[0], 1, requests.shape[1])
    wanted = lax.all_to_all(asked, "group", split_axis=0, concat_axis=0, tiled=True)
    core, parity = lax.axis_index("core"), lax.axis_index("zl")
    tables = task_tables(tasks, counts, core, parity, 2 * half, amount)
    blank = jnp.zeros((1, tile, tile), amplitudes.dtype)
    local = jnp.concatenate([amplitudes, blank, integrals])
    wanted, local = lax.optimization_barrier((wanted, local))
    fetched = lax.all_to_all(
        select(wanted, local, amount + 1), "group", split_axis=0, concat_axis=0, tiled=True
    )
    other = contract(0, tables, local, fetched, half, amount)
    other = lax.ppermute(other, "core", [(0, 1), (1, 0)])
    own = contract(1, tables, local, fetched, half, amount)
    return reduce_members(own, other)


def solution(mesh):
    finer = Mesh(mesh.devices.reshape(mesh.shape["group"], 8, 2, 2), GROUP_MEMBER)
    placed = (
        P(GROUP_MEMBER, None, None),
        P(GROUP_MEMBER, None, None),
        P(GROUP_MEMBER, None),
        P(GROUP_MEMBER, None),
        P(GROUP_MEMBER),
    )
    return jax.shard_map(
        per_device,
        mesh=finer,
        in_specs=placed,
        out_specs=P(GROUP_MEMBER, None, None),
        check_vma=False,
    )
```

```python
import functools

import jax
import jax.numpy as jnp
from jax import lax
from jax.experimental import pallas as pl
from jax.experimental.pallas import tpu as pltpu
from jax.sharding import Mesh
from jax.sharding import PartitionSpec as P

GROUP_MEMBER = ("group", "zh", "zl", "core")
Z = ("zh", "zl")
PAIR = 2

SLOTS = 512
TOP = 32760.0
SCALE_ROWS = 8
STEPS = 128.0


def select_kernel(base, me, wanted, local, out):
    rows, cap, _ = wanted.shape
    for i in range(rows):
        for c in range(cap):
            out[i * cap + c] = local[base + wanted[i, c, me[0]]]


def select(me, wanted, local, base):
    size = local.shape[1]
    slots = wanted.shape[0] * wanted.shape[1]
    full = lambda n: pl.BlockSpec((n, size, size), lambda i, *_: (0, 0, 0))
    return pl.pallas_call(
        functools.partial(select_kernel, base),
        grid_spec=pltpu.PrefetchScalarGridSpec(
            num_scalar_prefetch=2,
            grid=(1,),
            in_specs=[full(local.shape[0])],
            out_specs=full(slots),
        ),
        out_shape=jax.ShapeDtypeStruct((slots, size, size), local.dtype),
        compiler_params=pltpu.CompilerParams(vmem_limit_bytes=16 << 20),
        cost_estimate=pl.CostEstimate(flops=0, bytes_accessed=2 << 20, transcendentals=0),
        name="select",
    )(me, wanted, local)


def task_tables(tasks, counts, core, parity, tiles, blank):
    a, s, r = tasks.T
    half = tiles // 2
    k = jnp.arange(tasks.shape[0], dtype=jnp.int32)
    valid = k < counts[0]
    side = ((r & 1) ^ core ^ 1) * half + (((r >> 1) & 1) ^ parity ^ 1) * (half // 2) + (r >> 2)
    q = jnp.where(valid, side, tiles)
    code = a + s * 32
    rank = jnp.sum(((q[:, None] == q[None, :]) & (k[None, :] < k[:, None])).astype(jnp.int32), 1)
    b = jnp.arange(tiles, dtype=jnp.int32)
    hot = q[:, None] == b[None, :]
    groups = (jnp.sum(hot.astype(jnp.int32), 0) + PAIR - 1) // PAIR
    ends = jnp.sum(jnp.where(b[:, None] <= b[None, :], groups[:, None], 0), 0)
    first = jnp.sum(jnp.where(hot, (ends - groups)[None, :], 0), 1)
    place = jnp.where(valid, first * PAIR + rank, -1)
    p = jnp.arange(SLOTS, dtype=jnp.int32)
    table = blank + jnp.sum(jnp.where(place[:, None] == p[None, :], code[:, None] - blank, 0), 0)
    j = jnp.arange(SLOTS // PAIR, dtype=jnp.int32)
    target = jnp.sum((ends[:, None] <= j[None, :]).astype(jnp.int32), 0)
    return table, target, ends


def contract_kernel(first, count, unroll, blank, table, target, ends, amps, fetched, out):
    low = ends[first - 1] if first else 0
    high = ends[first + count - 1]
    out[...] = jnp.zeros_like(out)

    def step(i, carry):
        products = []
        for u in range(unroll):
            j = low + i * unroll + u
            codes = [jnp.where(j < high, table[j * PAIR + n], blank) for n in range(PAIR)]
            left = jnp.concatenate([amps[c & 31] for c in codes], axis=1)
            right = jnp.concatenate([fetched[c >> 5] for c in codes], axis=0)
            products.append(jnp.dot(left, right, preferred_element_type=jnp.float32))
        for u in range(unroll):
            j = low + i * unroll + u
            out[jnp.minimum(target[j] - first, count - 1)] += products[u]
        return carry

    lax.fori_loop(0, (high - low + unroll - 1) // unroll, step, 0)


def contract(first, count, unroll, tables, amps, fetched, blank):
    size = amps.shape[1]
    full = lambda n: pl.BlockSpec((n, size, size), lambda i, *_: (0, 0, 0))
    return pl.pallas_call(
        functools.partial(contract_kernel, first, count, unroll, blank),
        grid_spec=pltpu.PrefetchScalarGridSpec(
            num_scalar_prefetch=3,
            grid=(1,),
            in_specs=[full(amps.shape[0]), full(fetched.shape[0])],
            out_specs=full(count),
        ),
        out_shape=jax.ShapeDtypeStruct((count, size, size), jnp.float32),
        compiler_params=pltpu.CompilerParams(vmem_limit_bytes=16 << 20),
        cost_estimate=pl.CostEstimate(
            flops=1 << 32, bytes_accessed=4 << 20, transcendentals=0
        ),
        name="contract_%d" % first,
    )(*tables, amps, fetched)


def store_coded(v, out, i):
    rows = v.shape[0]
    top = jnp.max(jnp.abs(v), axis=0, keepdims=True)
    scale = jnp.ceil(jnp.log2(jnp.maximum(top, 1e-32)) * STEPS + 0.01)
    codes = v * (jnp.exp2(scale * (-1.0 / STEPS)) * TOP)
    out[i, :rows] = jnp.floor(codes + 0.5).astype(jnp.int32).astype(jnp.int16)
    row = jnp.broadcast_to(scale, (SCALE_ROWS, v.shape[1]))
    out[i, rows:] = row.astype(jnp.int32).astype(jnp.int16)


def load_coded(coded, i):
    rows = coded.shape[1] - SCALE_ROWS
    scale = coded[i, rows:].astype(jnp.int32).astype(jnp.float32)[:1]
    codes = coded[i, :rows].astype(jnp.int32).astype(jnp.float32)
    return codes * (jnp.exp2(scale * (1.0 / STEPS)) * (1.0 / TOP))


def plain_call(kernel, name, outs, *args):
    return pl.pallas_call(
        kernel,
        out_shape=outs,
        compiler_params=pltpu.CompilerParams(vmem_limit_bytes=8 << 20),
        cost_estimate=pl.CostEstimate(flops=1 << 20, bytes_accessed=2 << 20, transcendentals=0),
        name=name,
    )(*args)


def give_kernel(own, other, out):
    for i in range(out.shape[0]):
        store_coded(own[i] + other[i], out, i)


def take_kernel(own, other, arrived, out):
    for i in range(out.shape[0]):
        k = out.shape[0] + i
        store_coded(own[i] + other[k] + load_coded(arrived, i), out, i)


def finish_kernel(pieces, out):
    total = load_coded(pieces, 0)
    for i in range(1, pieces.shape[0]):
        total += load_coded(pieces, i)
    out[0] = total


def near_route(chips):
    route = []
    for z in range(chips):
        route.append((2 * z, 2 * (z ^ 1)))
        route.append((2 * z + 1, 2 * ((z + 1 if z % 2 else z - 1) % chips) + 1))
    return route


def per_device(amplitudes, integrals, tasks, requests, counts):
    amount, tile, _ = amplitudes.shape
    half = lax.axis_size(Z)
    asked = jnp.broadcast_to(requests.T, (requests.shape[0], *requests.T.shape))
    me = lax.axis_index("group").astype(jnp.int32).reshape(1)
    wanted = lax.all_to_all(asked, "group", split_axis=0, concat_axis=0, tiled=True)
    core, parity = lax.axis_index("core"), lax.axis_index("zl")
    tables = task_tables(tasks, counts, core, parity, 2 * half, amount)
    blank = jnp.zeros((1, tile, tile), amplitudes.dtype)
    local = jnp.concatenate([amplitudes, blank, integrals])
    wanted, tables, local = lax.optimization_barrier((wanted, tables, local))
    fetched = lax.all_to_all(
        select(me, wanted, local, amount + 1), "group", split_axis=0, concat_axis=0, tiled=True
    )
    part = half // 2
    coded = jax.ShapeDtypeStruct((part, tile + SCALE_ROWS, tile), jnp.int16)
    other = contract(0, half, 24, tables, local, fetched, amount)
    other = lax.ppermute(other, "core", [(0, 1), (1, 0)])
    own = contract(half, part, 16, tables, local, fetched, amount)
    away = plain_call(give_kernel, "give", coded, own, other)
    away, tables = lax.optimization_barrier((away, tables))
    arrived = lax.ppermute(away, (*Z, "core"), near_route(half))
    own = contract(half + part, part, 16, tables, local, fetched, amount)
    pieces = plain_call(take_kernel, "take", coded, own, other, arrived)
    pieces = lax.all_to_all(pieces, "zh", split_axis=0, concat_axis=0, tiled=True)
    total = jax.ShapeDtypeStruct((1, tile, tile), jnp.float32)
    return plain_call(finish_kernel, "finish", total, pieces)


def solution(mesh):
    finer = Mesh(mesh.devices.reshape(mesh.shape["group"], 8, 2, 2), GROUP_MEMBER)
    placed = (
        P(GROUP_MEMBER, None, None),
        P(GROUP_MEMBER, None, None),
        P(GROUP_MEMBER, None),
        P(GROUP_MEMBER, None),
        P(GROUP_MEMBER),
    )
    return jax.shard_map(
        per_device,
        mesh=finer,
        in_specs=placed,
        out_specs=P(GROUP_MEMBER, None, None),
        check_vma=False,
    )
```
